256 devices in a mesh: clus: 32 (over y, z), tgt: 8 (over x, core).
Axes of the slice: x: 4, y: 4, z: 8, core: 2. Of those that a mesh axis runs over, the one named last changes fastest.
Arguments:
- weights_init: float32 [262144, 1024], P('clus', 'tgt'), may hold values from -6 to 6
- margins: float32 [4096, 1024], P('clus', 'tgt')
- block_bits: int32 [9216, 128, 8], P('clus'), may hold values from 0 to 65535
- block_run_index: int32 [9216], P('clus'), may hold values from 0 to 31, as said below
- block_col: int32 [9216], P('clus'), may hold values from 0 to 63
- block_tally: int32 [32], P('clus'), may hold values from 144 to 288, as said below
- step_size: float32 [1], replicated, may hold values from 0.3 to 0.6
- penalty: float32 [1], replicated, may hold values from 0.3 to 0.8
Outputs:
- weights: float32 [262144, 1024], P('clus', 'tgt')
- run_loss: float32 [4096], P('clus')
The draws below stay inside these ranges and needn't reach their ends.
Inputs may be any that keep to these rules, and one draw needn't show every extreme that they name: `block_run_index`: A device's slots name distinct pairs of run block and cluster block. `block_tally`: some device's list is full in every draw.
All inputs are finite; a program needn't handle non-finite values.
Results may differ from the reference program's by a relative error of at most 0.0025.
Values may be sent and summed in bfloat16 or wider, within the bound.
No kernel may reach another device: no remote copies, remote signals or barrier semaphores. Data moves between devices by JAX's collectives and lax.ppermute only.
A program may use at most 128 MiB of HBM per device.

```python
import jax
import jax.numpy as jnp
from jax import lax

BLOCK_ENTRIES = 128
CLUS_DEV = 8192
TARGETS = 1024
NBLK = 288
ITERS = 2
CLUSTERS = 262144
RUNS = 4096
SLOTS = 9216
N_CLUS = 32


def layout_lists(key):
    base = jax.random.fold_in(key, 7)
    nblocks = CLUS_DEV // BLOCK_ENTRIES
    width = N_CLUS * nblocks
    keys = jax.random.split(base, N_CLUS)
    orders = jax.vmap(lambda single: jax.random.permutation(single, width))(keys)[:, :NBLK].astype(jnp.int32)
    reach = orders // nblocks
    offset = (reach - reach[:, :1] + N_CLUS) % N_CLUS
    column = orders % nblocks
    devices = jnp.arange(N_CLUS, dtype=jnp.int32)
    runs = (devices[:, None] + N_CLUS // 2 + offset) % N_CLUS
    counts = jax.random.randint(jax.random.fold_in(base, 1), (N_CLUS,), NBLK // 2, NBLK + 1).astype(jnp.int32)
    fullest = jax.random.randint(jax.random.fold_in(base, 2), (), 0, N_CLUS).astype(jnp.int32)
    counts = jnp.where(devices == fullest, NBLK, counts).astype(jnp.int32)
    return (runs.reshape(-1).astype(jnp.int32), column.reshape(-1).astype(jnp.int32), counts)


def draw_block_run_index(key, part):
    return layout_lists(key)[0]


def draw_block_col(key, part):
    return layout_lists(key)[1]


def draw_block_tally(key, part):
    return layout_lists(key)[2]


def draw_margins(key, part):
    scale = 1.0 + 2.0 * jnp.arange(TARGETS, dtype=jnp.float32) / TARGETS
    values = jax.random.normal(jax.random.fold_in(key, 11), (RUNS, TARGETS), jnp.float32) * scale[None, :]
    return values.astype(jnp.float32)


def with_ends(values, key, low, largest):
    longest = values.shape.index(max(values.shape))
    spots = []
    for shift in (0, 1):
        where = [jax.random.randint(jax.random.fold_in(key, axis), (), 0, length) for axis, length in enumerate(values.shape)]
        where[longest] = (where[longest] + shift) % values.shape[longest]
        spots.append(tuple(where))
    return values.at[spots[0]].set(low).at[spots[1]].set(largest)


def level_of(own_key, dims, cuts, least, high):
    gain = 1.0
    for dim, blocks in cuts:
        steps = jax.random.uniform(jax.random.fold_in(jax.random.fold_in(own_key, 6), dim), (blocks,), jnp.float32, least / len(cuts), high / len(cuts))
        gain = gain * jnp.repeat(jnp.exp(steps), dims[dim] // blocks).reshape((-1,) + (1,) * (len(dims) - 1 - dim))
    return gain


def scatter_about(stream_key, shape, spread, most, shards=(), kind=jnp.bfloat16):
    entries = spread * jax.random.normal(stream_key, shape, jnp.float32)
    if shards:
        entries = entries * level_of(stream_key, shape, shards, -0.22, 0.18)
    return jnp.clip(entries, -most, most).astype(kind)


def setup_inputs(seed: int = 0) -> dict:
    seeds = jax.random.split(jax.random.key(seed), 9)
    weights_init = scatter_about(seeds[0], (CLUSTERS, TARGETS), 1.0, 6.0, ((0, 32), (1, 8)), jnp.float32)
    margins = draw_margins(jax.random.fold_in(seeds[8], 71), 0)
    block_bits = with_ends(jax.random.randint(seeds[2], (SLOTS, BLOCK_ENTRIES, 8), 0, 65536), jax.random.fold_in(seeds[2], 1), 0, 65535).astype(jnp.int32)
    block_run_index = draw_block_run_index(jax.random.fold_in(seeds[8], 71), 0)
    block_col = draw_block_col(jax.random.fold_in(seeds[8], 71), 0)
    block_tally = draw_block_tally(jax.random.fold_in(seeds[8], 71), 0)
    step_size = jnp.clip(jax.random.uniform(seeds[6], (1,), jnp.float32, 0.3, 0.6), 0.3, 0.6)
    penalty = jnp.clip(jax.random.uniform(seeds[7], (1,), jnp.float32, 0.3, 0.8), 0.3, 0.8)
    return {"weights_init": weights_init, "margins": margins, "block_bits": block_bits, "block_run_index": block_run_index, "block_col": block_col, "block_tally": block_tally, "step_size": step_size, "penalty": penalty}


def unpack_signs(words):
    shifts = jnp.arange(16, dtype=jnp.int32)
    packed_flags = jnp.right_shift(words[..., None], shifts) & 1
    sign_values = (2 * packed_flags - 1).astype(jnp.float32)
    return sign_values.reshape(words.shape[:-1] + (BLOCK_ENTRIES,))


def reference(weights_init, margins, block_bits, block_run_index, block_col, block_tally, step_size, penalty):
    ndev = N_CLUS
    nblocks = CLUS_DEV // BLOCK_ENTRIES
    packed_flags = block_bits.reshape(ndev, NBLK, BLOCK_ENTRIES, 8)
    runs = block_run_index.reshape(ndev, NBLK)
    cols = block_col.reshape(ndev, NBLK)
    live_slots = (jnp.arange(NBLK, dtype=jnp.int32)[None, :] < block_tally[:, None]).astype(jnp.float32)
    eta = step_size[0]
    thresh = eta * penalty[0]
    current = weights_init
    loss = jnp.zeros((RUNS,), jnp.float32)
    for step in range(ITERS):
        current_b = current.astype(jnp.bfloat16).reshape(ndev, nblocks, BLOCK_ENTRIES, TARGETS)

        def forward(total, device):
            sign_values = unpack_signs(packed_flags[device]) * live_slots[device][:, None, None]
            selected_block = current_b[device][cols[device]].astype(jnp.float32)
            product_rows = jnp.einsum('srk,skt->srt', sign_values, selected_block)
            return total.at[runs[device]].add(product_rows), None

        total, unused = lax.scan(forward, jnp.zeros((ndev, BLOCK_ENTRIES, TARGETS), jnp.float32), jnp.arange(ndev, dtype=jnp.int32))
        pred = total.reshape(RUNS, TARGETS) / 128.0
        err = pred - margins
        loss = jnp.mean(err * err, axis=1)
        err_b = err.astype(jnp.bfloat16).reshape(ndev, BLOCK_ENTRIES, TARGETS)

        def backward(carry, device):
            sign_values = unpack_signs(packed_flags[device]) * live_slots[device][:, None, None]
            design_rows = err_b[runs[device]].astype(jnp.float32)
            part = jnp.einsum('srk,srt->skt', sign_values, design_rows)
            grad_dev = jnp.zeros((nblocks, BLOCK_ENTRIES, TARGETS), jnp.float32).at[cols[device]].add(part)
            return carry, grad_dev

        unused, grads = lax.scan(backward, jnp.float32(0.0), jnp.arange(ndev, dtype=jnp.int32))
        grad = grads.reshape(CLUSTERS, TARGETS) / 128.0
        moved = current - eta * grad
        current = jnp.sign(moved) * jnp.maximum(jnp.abs(moved) - thresh, 0.0)
    return current, loss
```

```python
import functools

import jax
import jax.numpy as jnp
from jax import lax
from jax.experimental import pallas as pl
from jax.experimental.pallas import tpu as pltpu
from jax.sharding import PartitionSpec as P


B = 128
TARGETS = 1024
NY = 4
NZ = 8
UNROLL = 4
CHUNK = 8
FAR = 2
MIB = 1024 * 1024
DZ_SLOT = (0, 2, 6, 5, 1, 3, 7, 4)


def shift(x, dy, dz):
    pairs = [
        (y * NZ + z, ((y + dy) % NY) * NZ + (z + dz) % NZ)
        for y in range(NY)
        for z in range(NZ)
    ]
    return lax.ppermute(x, "clus", pairs)


def build_lists(run, col, tally):
    slots = run.shape[0]
    nrun = NY * NZ
    me = lax.axis_index("clus")
    dy = (run // NZ - me // NZ) % NY
    dz = (run % NZ - me % NZ) % NZ
    place = jnp.zeros_like(dz)
    for k, s in enumerate(DZ_SLOT):
        place = place + jnp.where(dz == k, s, 0)
    ids = jnp.arange(slots, dtype=jnp.int32)
    live = ids < tally[0]
    rel = jnp.where(live, dy * NZ + place, nrun)
    blocks = jnp.arange(nrun, dtype=jnp.int32)
    hot = (rel[:, None] == blocks[None, :]).astype(jnp.int32)
    pairs = (jnp.sum(hot, axis=0) + 1) // 2
    before = (blocks[None, :] < blocks[:, None]).astype(jnp.int32)
    first = jnp.sum(before * pairs[None, :], axis=1)
    rank = jnp.sum(
        ((rel[None, :] == rel[:, None]) & (ids[None, :] < ids[:, None])).astype(jnp.int32), axis=1
    )
    pos = jnp.where(live, 2 * jnp.sum(hot * first[None, :], axis=1) + rank, -1)
    max_pairs = (slots + nrun) // 2 + UNROLL
    where = jnp.arange(2 * max_pairs, dtype=jnp.int32)
    code = ids + col * 512 + 32768
    codes = jnp.sum(jnp.where(where[:, None] == pos[None, :], code[None, :], 0), axis=1)
    last = first + pairs
    order = jnp.arange(max_pairs, dtype=jnp.int32)
    owner = jnp.sum((order[:, None] >= last[None, :]).astype(jnp.int32), axis=1)
    owner = jnp.minimum(owner, nrun - 1)
    bounds = jnp.concatenate([first[::NZ], jnp.sum(pairs)[None]])
    return codes.astype(jnp.int32), owner.astype(jnp.int32), bounds.astype(jnp.int32)


def unpack(bits_ref, masks, slot, mag):
    words = bits_ref[slot]
    parts = []
    for w in range(8):
        row = jnp.broadcast_to(words[w : w + 1, :], (16, B))
        parts.append(jnp.where((row & masks) != 0, mag, -mag).astype(jnp.bfloat16))
    return jnp.concatenate(parts, axis=0)


def bit_masks():
    return jnp.left_shift(jnp.int32(1), lax.broadcasted_iota(jnp.int32, (16, B), 0))


def load_pair(codes_ref, bits_ref, masks, q, high):
    signs, cols = [], []
    for h in range(2):
        code = codes_ref[2 * q + h]
        mag = jnp.where(q < high, lax.shift_right_logical(code, 15), 0).astype(jnp.float32)
        signs.append(unpack(bits_ref, masks, code & 511, mag))
        cols.append(lax.shift_right_logical(code, 9) & 63)
    return jnp.concatenate(signs, axis=0), cols


def each_pair(bounds_ref, group, body):
    low, high = bounds_ref[group], bounds_ref[group + 1]

    def step(k, carry):
        body([low + k * UNROLL + u for u in range(UNROLL)], high)
        return carry

    lax.fori_loop(0, (high - low + UNROLL - 1) // UNROLL, step, 0)


def forward(codes_ref, owner_ref, bounds_ref, bits_ref, cur_b, groups, outs):
    pl.run_scoped(
        functools.partial(
            forward_groups, codes_ref, owner_ref, bounds_ref, bits_ref, cur_b, groups, outs
        ),
        pltpu.VMEM((NZ, B, B), jnp.float32),
    )


def forward_groups(codes_ref, owner_ref, bounds_ref, bits_ref, cur_b, groups, outs, total):
    masks = bit_masks()
    for group, out in zip(groups, outs):
        total[...] = jnp.zeros_like(total)

        def body(qs, high):
            products = []
            for q in qs:
                signs, cols = load_pair(codes_ref, bits_ref, masks, q, high)
                left = jnp.concatenate([cur_b[cols[0]], cur_b[cols[1]]], axis=1)
                products.append(jnp.dot(left, signs, preferred_element_type=jnp.float32))
            for q, product in zip(qs, products):
                row = owner_ref[q] & (NZ - 1)
                total[row] = total[row] + product

        each_pair(bounds_ref, group, body)
        out[...] = total[...].astype(jnp.bfloat16)


def backward(codes_ref, owner_ref, bounds_ref, bits_ref, errs, grad):
    masks = bit_masks()
    grad[...] = jnp.zeros_like(grad)
    for group in range(NY):

        def body(qs, high):
            products, places = [], []
            for q in qs:
                signs, cols = load_pair(codes_ref, bits_ref, masks, q, high)
                row = errs[group][owner_ref[q] & (NZ - 1)]
                products.append(
                    lax.dot_general(
                        row, signs, (((1,), (1,)), ((), ())), preferred_element_type=jnp.float32
                    )
                )
                places.append(cols)
            for product, cols in zip(products, places):
                for h in range(2):
                    grad[cols[h]] = grad[cols[h]] + product[:, h * B : (h + 1) * B]

        each_pair(bounds_ref, group, body)


def shrunk(cur, grad, eta, thresh):
    moved = cur - eta * (grad * (1.0 / 128.0))
    return jnp.maximum(moved - thresh, 0.0) + jnp.minimum(moved + thresh, 0.0)


def chunk(ref, k):
    return ref.at[pl.ds(k * CHUNK, CHUNK)]


def first_kernel(codes, owner, bounds, bits, margins, w, far, cur_b, goal, buf, sems):
    nchunks = w.shape[0] // CHUNK
    for k in range(nchunks):
        pltpu.make_async_copy(chunk(w, k), chunk(buf, k), sems.at[k]).start()
    goal[...] = margins[...].T * 128.0

    def turn(k, carry):
        pltpu.make_async_copy(chunk(w, k), chunk(buf, k), sems.at[k]).wait()
        for u in range(CHUNK):
            j = k * CHUNK + u
            cur_b[j] = buf[j].T.astype(jnp.bfloat16)
        return carry

    lax.fori_loop(0, nchunks, turn, 0)
    forward(codes, owner, bounds, bits, cur_b, (FAR,), (far,))


def middle_kernel(
    codes, owner, bounds, step, pen, bits, e0, e1, e2, e3, w, far, cur_b, new, buf, grad, sem, sems
):
    nchunks = w.shape[0] // CHUNK
    load = pltpu.make_async_copy(w, buf, sem)
    load.start()
    backward(codes, owner, bounds, bits, (e0, e1, e2, e3), grad)
    load.wait()
    eta = step[0]
    thresh = eta * pen[0]

    def update(k, carry):
        for u in range(CHUNK):
            j = k * CHUNK + u
            block = shrunk(buf[j].T, grad[j], eta, thresh)
            grad[j] = block
            cur_b[j] = block.astype(jnp.bfloat16)
        pltpu.make_async_copy(chunk(grad, k), chunk(new, k), sems.at[k]).start()
        return carry

    lax.fori_loop(0, nchunks, update, 0)
    forward(codes, owner, bounds, bits, cur_b, (FAR,), (far,))
    for k in range(nchunks):
        pltpu.make_async_copy(chunk(grad, k), chunk(new, k), sems.at[k]).wait()


def near_kernel(codes, owner, bounds, bits, cur_b, p1, p3):
    forward(codes, owner, bounds, bits, cur_b, (1, 3), (p1, p3))


def own_kernel(codes, owner, bounds, bits, cur_b, p0):
    forward(codes, owner, bounds, bits, cur_b, (0,), (p0,))


def last_kernel(
    codes, owner, bounds, step, pen, bits, e0, e1, e2, e3, cur, out, buf, grad, sem, sems
):
    nchunks = cur.shape[0] // CHUNK
    load = pltpu.make_async_copy(cur, buf, sem)
    load.start()
    backward(codes, owner, bounds, bits, (e0, e1, e2, e3), grad)
    load.wait()
    eta = step[0]
    thresh = eta * pen[0]

    def update(k, carry):
        for u in range(CHUNK):
            j = k * CHUNK + u
            grad[j] = shrunk(buf[j], grad[j], eta, thresh).T
        pltpu.make_async_copy(chunk(grad, k), chunk(out, k), sems.at[k]).start()
        return carry

    lax.fori_loop(0, nchunks, update, 0)
    for k in range(nchunks):
        pltpu.make_async_copy(chunk(grad, k), chunk(out, k), sems.at[k]).wait()


def run_kernel(kernel, smem, vmem, hbm, outs, out_hbm, scratch, pairs):
    in_specs = [pl.BlockSpec(memory_space=pltpu.SMEM)] * len(smem)
    in_specs += [pl.BlockSpec(memory_space=pltpu.VMEM)] * len(vmem)
    in_specs += [pl.BlockSpec(memory_space=pltpu.HBM)] * len(hbm)
    out_specs = [pl.BlockSpec(memory_space=pltpu.VMEM)] * len(outs)
    out_specs += [pl.BlockSpec(memory_space=pltpu.HBM)] * len(out_hbm)
    return pl.pallas_call(
        kernel,
        out_shape=[jax.ShapeDtypeStruct(s, d) for s, d in (*outs, *out_hbm)],
        in_specs=in_specs,
        out_specs=out_specs,
        scratch_shapes=scratch,
        compiler_params=pltpu.CompilerParams(vmem_limit_bytes=(49 if hbm else 32) * MIB),
        cost_estimate=pl.CostEstimate(
            flops=pairs * 16 * B * B * B, bytes_accessed=4 * 1024 * 1024, transcendentals=0
        ),
    )(*smem, *vmem, *hbm)


def send_parts(lists, bits, cur_b, far):
    part = ((NZ, B, B), jnp.bfloat16)
    total = shift(far, 2, 0)
    one, three = run_kernel(near_kernel, lists, (bits, cur_b), (), [part] * 2, [], [], 80)
    up = shift(one, 1, 0)
    down = shift(three, 3, 0)
    (own,) = run_kernel(own_kernel, lists, (bits, cur_b), (), [part], [], [], 40)
    total = own.astype(jnp.float32) + total.astype(jnp.float32)
    return total + up.astype(jnp.float32) + down.astype(jnp.float32)


def reduce_runs(total, goal):
    low = total.astype(jnp.bfloat16)
    mine = total[0:2]
    for dz, at in ((2, 6), (1, 2), (7, 4)):
        mine = mine + shift(low[at : at + 2], 0, dz).astype(jnp.float32)
    mine = jnp.stack([mine[0] - goal, mine[1]])
    other = shift(jnp.flip(mine, 0).astype(jnp.bfloat16), 0, 4)
    return (mine + other.astype(jnp.float32)) * (1.0 / 128.0)


def gather_runs(two):
    eight = jnp.concatenate([two, shift(two, 0, 7), shift(two, 0, 1), shift(two, 0, 6)])
    return [eight, shift(eight, 3, 0), shift(eight, 2, 0), shift(eight, 1, 0)]


def per_device(weights_init, margins, block_bits, run, col, tally, step_size, penalty):
    nblocks = weights_init.shape[0] // B
    bits = block_bits.transpose(0, 2, 1)
    lists = build_lists(run, col, tally)
    weights = weights_init.reshape(nblocks, B, B)
    part = ((NZ, B, B), jnp.bfloat16)
    table = ((nblocks, B, B), jnp.float32)
    table_b = ((nblocks, B, B), jnp.bfloat16)
    buffer = pltpu.VMEM(*table)
    single = pltpu.SemaphoreType.DMA
    many = pltpu.SemaphoreType.DMA((nblocks // CHUNK,))

    far, cur_b, goal = run_kernel(
        first_kernel,
        lists,
        (bits, margins),
        (weights,),
        [part, table_b, ((B, B), jnp.float32)],
        [],
        [buffer, many],
        80,
    )
    err = reduce_runs(send_parts(lists, bits, cur_b, far), goal)
    errs = gather_runs(err.astype(jnp.bfloat16))
    far, cur_b, cur = run_kernel(
        middle_kernel,
        (*lists, step_size, penalty),
        (bits, *errs),
        (weights,),
        [part, table_b],
        [table],
        [buffer, buffer, single, many],
        240,
    )
    err = reduce_runs(send_parts(lists, bits, cur_b, far), goal)
    errs = gather_runs(err.astype(jnp.bfloat16))
    squares = jnp.sum(err[0] * err[0], axis=0)
    for hop in (1, 2, 4):
        squares = squares + lax.ppermute(squares, "tgt", [(k, k ^ hop) for k in range(8)])
    (out,) = run_kernel(
        last_kernel,
        (*lists, step_size, penalty),
        (bits, *errs),
        (cur,),
        [],
        [table],
        [buffer, buffer, single, many],
        200,
    )
    return out.reshape(weights_init.shape), squares / TARGETS


def solution(mesh):
    return jax.shard_map(
        per_device,
        mesh=mesh,
        in_specs=(
            P("clus", "tgt"),
            P("clus", "tgt"),
            P("clus", None, None),
            P("clus"),
            P("clus"),
            P("clus"),
            P(),
            P(),
        ),
        out_specs=(P("clus", "tgt"), P("clus")),
        check_vma=False,
    )
```

```python
import functools

import jax
import jax.numpy as jnp
from jax import lax
from jax.experimental import pallas as pl
from jax.experimental.pallas import tpu as pltpu
from jax.sharding import PartitionSpec as P


B = 128
TARGETS = 1024
NY = 4
NZ = 8
UNROLL = 8
CHUNK = 8
FAR = 2
MIB = 1024 * 1024
DZ_SLOT = (0, 2, 6, 5, 1, 3, 7, 4)


def shift(x, dy, dz):
    pairs = [
        (y * NZ + z, ((y + dy) % NY) * NZ + (z + dz) % NZ)
        for y in range(NY)
        for z in range(NZ)
    ]
    return lax.ppermute(x, "clus", pairs)


def build_lists(run, col, tally):
    slots = run.shape[0]
    nrun = NY * NZ
    me = lax.axis_index("clus")
    dy = (run // NZ - me // NZ) % NY
    dz = (run % NZ - me % NZ) % NZ
    place = jnp.zeros_like(dz)
    for k, s in enumerate(DZ_SLOT):
        place = place + jnp.where(dz == k, s, 0)
    ids = jnp.arange(slots, dtype=jnp.int32)
    live = ids < tally[0]
    rel = jnp.where(live, dy * NZ + place, nrun)
    blocks = jnp.arange(nrun, dtype=jnp.int32)
    hot = (rel[:, None] == blocks[None, :]).astype(jnp.int32)
    pairs = (jnp.sum(hot, axis=0) + 1) // 2
    before = (blocks[None, :] < blocks[:, None]).astype(jnp.int32)
    first = jnp.sum(before * pairs[None, :], axis=1)
    rank = jnp.sum(
        ((rel[None, :] == rel[:, None]) & (ids[None, :] < ids[:, None])).astype(jnp.int32), axis=1
    )
    pos = jnp.where(live, 2 * jnp.sum(hot * first[None, :], axis=1) + rank, -1)
    max_pairs = (slots + nrun) // 2 + UNROLL
    where = jnp.arange(2 * max_pairs, dtype=jnp.int32)
    code = ids + col * 512 + 32768
    codes = jnp.sum(jnp.where(where[:, None] == pos[None, :], code[None, :], 0), axis=1)
    last = first + pairs
    order = jnp.arange(max_pairs, dtype=jnp.int32)
    owner = jnp.sum((order[:, None] >= last[None, :]).astype(jnp.int32), axis=1)
    owner = jnp.minimum(owner, nrun - 1)
    bounds = jnp.concatenate([first[::NZ], jnp.sum(pairs)[None]])
    return codes.astype(jnp.int32), owner.astype(jnp.int32), bounds.astype(jnp.int32)


def unpack(bits_ref, masks, slot, mag):
    words = bits_ref[slot]
    parts = []
    for w in range(8):
        row = jnp.broadcast_to(words[w : w + 1, :], (16, B))
        parts.append(jnp.where((row & masks) != 0, mag, -mag).astype(jnp.bfloat16))
    return jnp.concatenate(parts, axis=0)


def bit_masks():
    return jnp.left_shift(jnp.int32(1), lax.broadcasted_iota(jnp.int32, (16, B), 0))


def load_pair(codes_ref, bits_ref, masks, q, high):
    signs, cols = [], []
    for h in range(2):
        code = codes_ref[2 * q + h]
        mag = jnp.where(q < high, lax.shift_right_logical(code, 15), 0).astype(jnp.float32)
        signs.append(unpack(bits_ref, masks, code & 511, mag))
        cols.append(lax.shift_right_logical(code, 9) & 63)
    return jnp.concatenate(signs, axis=0), cols


def each_pair(bounds_ref, first, last, body):
    low, high = bounds_ref[first], bounds_ref[last]

    def step(k, carry):
        body([low + k * UNROLL + u for u in range(UNROLL)], high)
        return carry

    lax.fori_loop(0, (high - low + UNROLL - 1) // UNROLL, step, 0)


def forward(codes_ref, owner_ref, bounds_ref, bits_ref, cur_b, groups, outs):
    pl.run_scoped(
        functools.partial(
            forward_groups, codes_ref, owner_ref, bounds_ref, bits_ref, cur_b, groups, outs
        ),
        pltpu.VMEM((NZ, B, B), jnp.float32),
    )


def forward_groups(codes_ref, owner_ref, bounds_ref, bits_ref, cur_b, groups, outs, total):
    masks = bit_masks()
    for group, out in zip(groups, outs):
        total[...] = jnp.zeros_like(total)

        def body(qs, high):
            products = []
            for q in qs:
                signs, cols = load_pair(codes_ref, bits_ref, masks, q, high)
                products.append(
                    jnp.dot(cur_b[cols[0]], signs[:B], preferred_element_type=jnp.float32)
                    + jnp.dot(cur_b[cols[1]], signs[B:], preferred_element_type=jnp.float32)
                )
            for q, product in zip(qs, products):
                row = owner_ref[q] & (NZ - 1)
                total[row] = total[row] + product

        each_pair(bounds_ref, group, group + 1, body)
        out[...] = total[...].astype(jnp.bfloat16)


def backward(codes_ref, owner_ref, bounds_ref, bits_ref, errs, table, grad):
    masks = bit_masks()
    grad[...] = jnp.zeros_like(grad)
    for group in range(NY):
        table[group * NZ : (group + 1) * NZ] = errs[group][...]

    def body(qs, high):
        products, places = [], []
        for q in qs:
            signs, cols = load_pair(codes_ref, bits_ref, masks, q, high)
            row = table[owner_ref[q]]
            products.append(jnp.dot(signs, row, preferred_element_type=jnp.float32))
            places.append(cols)
        for product, cols in zip(products, places):
            for h in range(2):
                grad[cols[h]] = grad[cols[h]] + product[h * B : (h + 1) * B]

    each_pair(bounds_ref, 0, NY, body)


def shrunk(cur, grad, scale, thresh):
    moved = cur - scale * grad
    return moved - jnp.maximum(jnp.minimum(moved, thresh), -thresh)


def chunk(ref, k):
    return ref.at[pl.ds(k * CHUNK, CHUNK)]


def first_kernel(codes, owner, bounds, bits, w, far, cur_b, buf, sems):
    nchunks = w.shape[0] // CHUNK
    for k in range(nchunks):
        pltpu.make_async_copy(chunk(w, k), chunk(buf, k), sems.at[k]).start()

    def turn(k, carry):
        pltpu.make_async_copy(chunk(w, k), chunk(buf, k), sems.at[k]).wait()
        for u in range(CHUNK):
            j = k * CHUNK + u
            cur_b[j] = buf[j].astype(jnp.bfloat16).T
        return carry

    lax.fori_loop(0, nchunks, turn, 0)
    forward(codes, owner, bounds, bits, cur_b, (FAR,), (far,))


def middle_kernel(
    codes, owner, bounds, step, pen, bits, e0, e1, e2, e3, w, far, cur_b, new, buf, grad, table, sem, sems
):
    nchunks = w.shape[0] // CHUNK
    load = pltpu.make_async_copy(w, buf, sem)
    load.start()
    backward(codes, owner, bounds, bits, (e0, e1, e2, e3), table, grad)
    load.wait()
    scale = step[0] * (1.0 / 128.0)
    thresh = step[0] * pen[0]

    def update(k, carry):
        for u in range(CHUNK):
            j = k * CHUNK + u
            block = shrunk(buf[j], grad[j], scale, thresh)
            grad[j] = block
            cur_b[j] = block.astype(jnp.bfloat16).T
        pltpu.make_async_copy(chunk(grad, k), chunk(new, k), sems.at[k]).start()
        return carry

    lax.fori_loop(0, nchunks, update, 0)
    forward(codes, owner, bounds, bits, cur_b, (FAR,), (far,))
    for k in range(nchunks):
        pltpu.make_async_copy(chunk(grad, k), chunk(new, k), sems.at[k]).wait()


def err_kernel(mine, other, err, squares):
    both = (mine[...] + other[...].astype(jnp.float32)) * (1.0 / 128.0)
    squares[...] = jnp.sum(both[0] * both[0], axis=0, keepdims=True)
    for k in range(2):
        err[k] = both[k].T.astype(jnp.bfloat16)


def near_kernel(codes, owner, bounds, bits, cur_b, p1, p3):
    forward(codes, owner, bounds, bits, cur_b, (1, 3), (p1, p3))


def own_kernel(codes, owner, bounds, bits, cur_b, p0):
    forward(codes, owner, bounds, bits, cur_b, (0,), (p0,))


def own_goal_kernel(codes, owner, bounds, bits, cur_b, margins, p0, goal):
    goal[...] = margins[...].T * 128.0
    forward(codes, owner, bounds, bits, cur_b, (0,), (p0,))


def last_kernel(
    codes, owner, bounds, step, pen, bits, e0, e1, e2, e3, cur, out, buf, grad, table, sem, sems
):
    nchunks = cur.shape[0] // CHUNK
    load = pltpu.make_async_copy(cur, buf, sem)
    load.start()
    backward(codes, owner, bounds, bits, (e0, e1, e2, e3), table, grad)
    load.wait()
    scale = step[0] * (1.0 / 128.0)
    thresh = step[0] * pen[0]

    def update(k, carry):
        for u in range(CHUNK):
            j = k * CHUNK + u
            grad[j] = shrunk(buf[j], grad[j], scale, thresh)
        pltpu.make_async_copy(chunk(grad, k), chunk(out, k), sems.at[k]).start()
        return carry

    lax.fori_loop(0, nchunks, update, 0)
    for k in range(nchunks):
        pltpu.make_async_copy(chunk(grad, k), chunk(out, k), sems.at[k]).wait()


def run_kernel(kernel, smem, vmem, hbm, outs, out_hbm, scratch, pairs, grant=32):
    in_specs = [pl.BlockSpec(memory_space=pltpu.SMEM)] * len(smem)
    in_specs += [pl.BlockSpec(memory_space=pltpu.VMEM)] * len(vmem)
    in_specs += [pl.BlockSpec(memory_space=pltpu.HBM)] * len(hbm)
    out_specs = [pl.BlockSpec(memory_space=pltpu.VMEM)] * len(outs)
    out_specs += [pl.BlockSpec(memory_space=pltpu.HBM)] * len(out_hbm)
    return pl.pallas_call(
        kernel,
        out_shape=[jax.ShapeDtypeStruct(s, d) for s, d in (*outs, *out_hbm)],
        in_specs=in_specs,
        out_specs=out_specs,
        scratch_shapes=scratch,
        compiler_params=pltpu.CompilerParams(vmem_limit_bytes=grant * MIB),
        cost_estimate=pl.CostEstimate(
            flops=pairs * 16 * B * B * B, bytes_accessed=4 * 1024 * 1024, transcendentals=0
        ),
    )(*smem, *vmem, *hbm)


def send_parts(lists, bits, cur_b, far, margins=None):
    part = ((NZ, B, B), jnp.bfloat16)
    total = shift(far, 2, 0)
    one, three = run_kernel(near_kernel, lists, (bits, cur_b), (), [part] * 2, [], [], 80)
    up = shift(one, 1, 0)
    down = shift(three, 3, 0)
    kernel, more, outs = own_kernel, (), [part]
    if margins is not None:
        kernel, more, outs = own_goal_kernel, (margins,), [part, ((B, B), jnp.float32)]
    own, *goal = run_kernel(kernel, lists, (bits, cur_b, *more), (), outs, [], [], 40)
    total = own.astype(jnp.float32) + total.astype(jnp.float32)
    return total + up.astype(jnp.float32) + down.astype(jnp.float32), *goal


def reduce_runs(total, goal):
    low = total.astype(jnp.bfloat16)
    mine = total[0:2]
    for dz, at in ((2, 6), (1, 2), (7, 4)):
        mine = mine + shift(low[at : at + 2], 0, dz).astype(jnp.float32)
    mine = jnp.stack([mine[0] - goal, mine[1]])
    other = shift(jnp.flip(mine, 0).astype(jnp.bfloat16), 0, 4)
    pair = ((2, B, B), jnp.bfloat16)
    err, squares = run_kernel(
        err_kernel, (), (mine, other), (), [pair, ((1, B), jnp.float32)], [], [], 1
    )
    return err, squares


def gather_runs(two):
    eight = jnp.concatenate([two, shift(two, 0, 7), shift(two, 0, 1), shift(two, 0, 6)])
    return [eight, shift(eight, 3, 0), shift(eight, 2, 0), shift(eight, 1, 0)]


def per_device(weights_init, margins, block_bits, run, col, tally, step_size, penalty):
    nblocks = weights_init.shape[0] // B
    bits = block_bits.transpose(0, 2, 1)
    lists = build_lists(run, col, tally)
    weights = weights_init.reshape(nblocks, B, B)
    part = ((NZ, B, B), jnp.bfloat16)
    table = ((nblocks, B, B), jnp.float32)
    table_b = ((nblocks, B, B), jnp.bfloat16)
    buffer = pltpu.VMEM(*table)
    err_table = pltpu.VMEM((NY * NZ, B, B), jnp.bfloat16)
    single = pltpu.SemaphoreType.DMA
    many = pltpu.SemaphoreType.DMA((nblocks // CHUNK,))

    far, cur_b = run_kernel(
        first_kernel, lists, (bits,), (weights,), [part, table_b], [], [buffer, many], 80, 49
    )
    total, goal = send_parts(lists, bits, cur_b, far, margins)
    err, _ = reduce_runs(total, goal)
    errs = gather_runs(err)
    far, cur_b, cur = run_kernel(
        middle_kernel,
        (*lists, step_size, penalty),
        (bits, *errs),
        (weights,),
        [part, table_b],
        [table],
        [buffer, buffer, err_table, single, many],
        240,
        49,
    )
    (total,) = send_parts(lists, bits, cur_b, far)
    err, squares = reduce_runs(total, goal)
    errs = gather_runs(err)
    squares = squares.reshape(B)
    for hop in (1, 2, 4):
        squares = squares + lax.ppermute(squares, "tgt", [(k, k ^ hop) for k in range(8)])
    (out,) = run_kernel(
        last_kernel,
        (*lists, step_size, penalty),
        (bits, *errs),
        (cur,),
        [],
        [table],
        [buffer, buffer, err_table, single, many],
        200,
        49,
    )
    return out.reshape(weights_init.shape), squares / TARGETS


def solution(mesh):
    return jax.shard_map(
        per_device,
        mesh=mesh,
        in_specs=(
            P("clus", "tgt"),
            P("clus", "tgt"),
            P("clus", None, None),
            P("clus"),
            P("clus"),
            P("clus"),
            P(),
            P(),
        ),
        out_specs=(P("clus", "tgt"), P("clus")),
        check_vma=False,
    )
```

```python
import functools

import jax
import jax.numpy as jnp
from jax import lax
from jax.experimental import pallas as pl
from jax.experimental.pallas import tpu as pltpu
from jax.sharding import PartitionSpec as P


B = 128
TARGETS = 1024
NY = 4
NZ = 8
UNROLL = 8
PAD = 8
CHUNK = 8
FAR = 2
MIB = 1024 * 1024
DZ_SLOT = (0, 2, 6, 5, 1, 3, 7, 4)


def shift(x, dy, dz):
    pairs = [
        (y * NZ + z, ((y + dy) % NY) * NZ + (z + dz) % NZ)
        for y in range(NY)
        for z in range(NZ)
    ]
    return lax.ppermute(x, "clus", pairs)


def build_lists(run, col, tally):
    slots = run.shape[0]
    nrun = NY * NZ
    me = lax.axis_index("clus")
    dy = (run // NZ - me // NZ) % NY
    dz = (run % NZ - me % NZ) % NZ
    place = jnp.zeros_like(dz)
    for k, s in enumerate(DZ_SLOT):
        place = place + jnp.where(dz == k, s, 0)
    ids = jnp.arange(slots, dtype=jnp.int32)
    live = ids < tally[0]
    rel = jnp.where(live, dy * NZ + place, nrun)
    blocks = jnp.arange(nrun, dtype=jnp.int32)
    hot = (rel[:, None] == blocks[None, :]).astype(jnp.int32)
    pairs = (jnp.sum(hot, axis=0) + 1) // 2
    before = (blocks[None, :] < blocks[:, None]).astype(jnp.int32)
    first = jnp.sum(before * pairs[None, :], axis=1)
    rank = jnp.sum(
        ((rel[None, :] == rel[:, None]) & (ids[None, :] < ids[:, None])).astype(jnp.int32), axis=1
    )
    pos = jnp.where(live, 2 * jnp.sum(hot * first[None, :], axis=1) + rank, -1)
    max_pairs = (slots + nrun) // 2 + UNROLL
    where = jnp.arange(2 * max_pairs, dtype=jnp.int32)
    code = ids + col * 512 + 32768
    codes = jnp.sum(jnp.where(where[:, None] == pos[None, :], code[None, :], 0), axis=1)
    last = first + pairs
    order = jnp.arange(max_pairs + PAD, dtype=jnp.int32)
    group_start = NZ * (order - max_pairs)
    terms = jnp.where(
        order[:, None] < max_pairs,
        (order[:, None] >= last[None, :]).astype(jnp.int32),
        jnp.where(blocks[None, :] < group_start[:, None], pairs[None, :], 0),
    )
    return codes.astype(jnp.int32), jnp.sum(terms, axis=1).astype(jnp.int32)


def unpack(bits_ref, masks, slot, mag):
    words = bits_ref[slot]
    parts = []
    for w in range(8):
        row = jnp.broadcast_to(words[w : w + 1, :], (16, B))
        parts.append(jnp.where((row & masks) != 0, mag, -mag).astype(jnp.bfloat16))
    return jnp.concatenate(parts, axis=0)


def bit_masks():
    return jnp.left_shift(jnp.int32(1), lax.broadcasted_iota(jnp.int32, (16, B), 0))


def load_pair(codes_ref, bits_ref, masks, q, high):
    signs, cols = [], []
    for h in range(2):
        code = codes_ref[2 * q + h]
        mag = jnp.where(q < high, lax.shift_right_logical(code, 15), 0).astype(jnp.float32)
        signs.append(unpack(bits_ref, masks, code & 511, mag))
        cols.append(lax.shift_right_logical(code, 9) & 63)
    return jnp.concatenate(signs, axis=0), cols


def each_pair(owner_ref, first, last, body):
    base = owner_ref.shape[0] - PAD
    low, high = owner_ref[base + first], owner_ref[base + last]

    def step(k, carry):
        body([low + k * UNROLL + u for u in range(UNROLL)], high)
        return carry

    lax.fori_loop(0, (high - low + UNROLL - 1) // UNROLL, step, 0)


def forward(codes_ref, owner_ref, bits_ref, cur_b, groups, outs):
    pl.run_scoped(
        functools.partial(
            forward_groups, codes_ref, owner_ref, bits_ref, cur_b, groups, outs
        ),
        pltpu.VMEM((NZ, B, B), jnp.float32),
    )


def forward_groups(codes_ref, owner_ref, bits_ref, cur_b, groups, outs, total):
    masks = bit_masks()
    for group, out in zip(groups, outs):
        total[...] = jnp.zeros_like(total)

        def body(qs, high):
            products = []
            for q in qs:
                signs, cols = load_pair(codes_ref, bits_ref, masks, q, high)
                products.append(
                    jnp.dot(cur_b[cols[0]], signs[:B], preferred_element_type=jnp.float32)
                    + jnp.dot(cur_b[cols[1]], signs[B:], preferred_element_type=jnp.float32)
                )
            for q, product in zip(qs, products):
                row = owner_ref[q] & (NZ - 1)
                total[row] = total[row] + product

        each_pair(owner_ref, group, group + 1, body)
        out[...] = total[...].astype(jnp.bfloat16)


def backward(codes_ref, owner_ref, bits_ref, errs, table, grad):
    masks = bit_masks()
    grad[...] = jnp.zeros_like(grad)
    for group in range(NY):
        table[group * NZ : (group + 1) * NZ] = errs[group][...]

    def body(qs, high):
        products, places = [], []
        for q in qs:
            signs, cols = load_pair(codes_ref, bits_ref, masks, q, high)
            row = table[owner_ref[q] & (NY * NZ - 1)]
            products.append(jnp.dot(signs, row, preferred_element_type=jnp.float32))
            places.append(cols)
        for product, cols in zip(products, places):
            for h in range(2):
                grad[cols[h]] = grad[cols[h]] + product[h * B : (h + 1) * B]

    each_pair(owner_ref, 0, NY, body)


def shrunk(cur, grad, scale, thresh):
    moved = cur - scale * grad
    return moved - jnp.maximum(jnp.minimum(moved, thresh), -thresh)


def chunk(ref, k):
    return ref.at[pl.ds(k * CHUNK, CHUNK)]


def first_kernel(codes, owner, bits, w, far, cur_b, buf, sems):
    nchunks = w.shape[0] // CHUNK
    for k in range(nchunks):
        pltpu.make_async_copy(chunk(w, k), chunk(buf, k), sems.at[k]).start()

    def turn(k, carry):
        pltpu.make_async_copy(chunk(w, k), chunk(buf, k), sems.at[k]).wait()
        for u in range(CHUNK):
            j = k * CHUNK + u
            cur_b[j] = buf[j].astype(jnp.bfloat16).T
        return carry

    lax.fori_loop(0, nchunks, turn, 0)
    forward(codes, owner, bits, cur_b, (FAR,), (far,))


def middle_kernel(
    codes, owner, step, pen, bits, e0, e1, e2, e3, w, far, cur_b, new, buf, grad, table, sem, sems
):
    nchunks = w.shape[0] // CHUNK
    load = pltpu.make_async_copy(w, buf, sem)
    load.start()
    backward(codes, owner, bits, (e0, e1, e2, e3), table, grad)
    load.wait()
    scale = step[0] * (1.0 / 128.0)
    thresh = step[0] * pen[0]

    def update(k, carry):
        for u in range(CHUNK):
            j = k * CHUNK + u
            block = shrunk(buf[j], grad[j], scale, thresh)
            grad[j] = block
            cur_b[j] = block.astype(jnp.bfloat16).T
        pltpu.make_async_copy(chunk(grad, k), chunk(new, k), sems.at[k]).start()
        return carry

    lax.fori_loop(0, nchunks, update, 0)
    forward(codes, owner, bits, cur_b, (FAR,), (far,))
    for k in range(nchunks):
        pltpu.make_async_copy(chunk(grad, k), chunk(new, k), sems.at[k]).wait()


def err_kernel(mine, other, err, squares):
    both = (mine[...] + other[...].astype(jnp.float32)) * (1.0 / 128.0)
    squares[...] = jnp.sum(both[0] * both[0], axis=0, keepdims=True)
    for k in range(2):
        err[k] = both[k].T.astype(jnp.bfloat16)


def near_kernel(codes, owner, bits, cur_b, p1, p3):
    forward(codes, owner, bits, cur_b, (1, 3), (p1, p3))


def own_kernel(codes, owner, bits, cur_b, p0):
    forward(codes, owner, bits, cur_b, (0,), (p0,))


def own_goal_kernel(codes, owner, bits, cur_b, margins, p0, goal):
    goal[...] = margins[...].T * 128.0
    forward(codes, owner, bits, cur_b, (0,), (p0,))


def last_kernel(
    codes, owner, step, pen, bits, e0, e1, e2, e3, cur, out, buf, grad, table, sem, sems
):
    nchunks = cur.shape[0] // CHUNK
    load = pltpu.make_async_copy(cur, buf, sem)
    load.start()
    backward(codes, owner, bits, (e0, e1, e2, e3), table, grad)
    load.wait()
    scale = step[0] * (1.0 / 128.0)
    thresh = step[0] * pen[0]

    def update(k, carry):
        for u in range(CHUNK):
            j = k * CHUNK + u
            grad[j] = shrunk(buf[j], grad[j], scale, thresh)
        pltpu.make_async_copy(chunk(grad, k), chunk(out, k), sems.at[k]).start()
        return carry

    lax.fori_loop(0, nchunks, update, 0)
    for k in range(nchunks):
        pltpu.make_async_copy(chunk(grad, k), chunk(out, k), sems.at[k]).wait()


def run_kernel(kernel, smem, vmem, hbm, outs, out_hbm, scratch, pairs, grant=32):
    in_specs = [pl.BlockSpec(memory_space=pltpu.SMEM)] * len(smem)
    in_specs += [pl.BlockSpec(memory_space=pltpu.VMEM)] * len(vmem)
    in_specs += [pl.BlockSpec(memory_space=pltpu.HBM)] * len(hbm)
    out_specs = [pl.BlockSpec(memory_space=pltpu.VMEM)] * len(outs)
    out_specs += [pl.BlockSpec(memory_space=pltpu.HBM)] * len(out_hbm)
    return pl.pallas_call(
        kernel,
        out_shape=[jax.ShapeDtypeStruct(s, d) for s, d in (*outs, *out_hbm)],
        in_specs=in_specs,
        out_specs=out_specs,
        scratch_shapes=scratch,
        compiler_params=pltpu.CompilerParams(vmem_limit_bytes=grant * MIB),
        cost_estimate=pl.CostEstimate(
            flops=pairs * 16 * B * B * B, bytes_accessed=4 * 1024 * 1024, transcendentals=0
        ),
    )(*smem, *vmem, *hbm)


def send_parts(lists, bits, cur_b, far, margins=None):
    part = ((NZ, B, B), jnp.bfloat16)
    total = shift(far, 2, 0)
    one, three = run_kernel(near_kernel, lists, (bits, cur_b), (), [part] * 2, [], [], 80)
    up = shift(one, 1, 0)
    down = shift(three, 3, 0)
    kernel, more, outs = own_kernel, (), [part]
    if margins is not None:
        kernel, more, outs = own_goal_kernel, (margins,), [part, ((B, B), jnp.float32)]
    own, *goal = run_kernel(kernel, lists, (bits, cur_b, *more), (), outs, [], [], 40)
    total = own.astype(jnp.float32) + total.astype(jnp.float32)
    return total + up.astype(jnp.float32) + down.astype(jnp.float32), *goal


def reduce_runs(total, goal):
    low = total.astype(jnp.bfloat16)
    mine = total[0:2]
    for dz, at in ((2, 6), (1, 2), (7, 4)):
        mine = mine + shift(low[at : at + 2], 0, dz).astype(jnp.float32)
    mine = jnp.stack([mine[0] - goal, mine[1]])
    other = shift(jnp.flip(mine, 0).astype(jnp.bfloat16), 0, 4)
    pair = ((2, B, B), jnp.bfloat16)
    err, squares = run_kernel(
        err_kernel, (), (mine, other), (), [pair, ((1, B), jnp.float32)], [], [], 1
    )
    return err, squares


def gather_runs(two):
    eight = jnp.concatenate([two, shift(two, 0, 7), shift(two, 0, 1), shift(two, 0, 6)])
    parts = [eight]
    for dy in (3, 2, 1):
        parts.append(shift(eight, dy, 0))
    return parts


def per_device(weights_init, margins, block_bits, run, col, tally, step_size, penalty):
    nblocks = weights_init.shape[0] // B
    bits = block_bits.transpose(0, 2, 1)
    lists = build_lists(run, col, tally)
    weights = weights_init.reshape(nblocks, B, B)
    part = ((NZ, B, B), jnp.bfloat16)
    table = ((nblocks, B, B), jnp.float32)
    table_b = ((nblocks, B, B), jnp.bfloat16)
    buffer = pltpu.VMEM(*table)
    err_table = pltpu.VMEM((NY * NZ, B, B), jnp.bfloat16)
    single = pltpu.SemaphoreType.DMA
    many = pltpu.SemaphoreType.DMA((nblocks // CHUNK,))

    far, cur_b = run_kernel(
        first_kernel, lists, (bits,), (weights,), [part, table_b], [], [buffer, many], 80, 49
    )
    total, goal = send_parts(lists, bits, cur_b, far, margins)
    err, _ = reduce_runs(total, goal)
    errs = gather_runs(err)
    far, cur_b, cur = run_kernel(
        middle_kernel,
        (*lists, step_size, penalty),
        (bits, *errs),
        (weights,),
        [part, table_b],
        [table],
        [buffer, buffer, err_table, single, many],
        240,
        49,
    )
    (total,) = send_parts(lists, bits, cur_b, far)
    err, squares = reduce_runs(total, goal)
    errs = gather_runs(err)
    squares = squares.reshape(B)
    squares = squares + lax.ppermute(squares, "tgt", [(k, k ^ 1) for k in range(8)])
    others = []
    for step in (2, 4, 6):
        others.append(
            lax.ppermute(squares, "tgt", [(k, (k + step) % 8) for k in range(8)])
        )
    squares = (squares + others[1]) + (others[0] + others[2])
    (out,) = run_kernel(
        last_kernel,
        (*lists, step_size, penalty),
        (bits, *errs),
        (cur,),
        [],
        [table],
        [buffer, buffer, err_table, single, many],
        200,
        49,
    )
    return out.reshape(weights_init.shape), squares / TARGETS


def solution(mesh):
    return jax.shard_map(
        per_device,
        mesh=mesh,
        in_specs=(
            P("clus", "tgt"),
            P("clus", "tgt"),
            P("clus", None, None),
            P("clus"),
            P("clus"),
            P("clus"),
            P(),
            P(),
        ),
        out_specs=(P("clus", "tgt"), P("clus")),
        check_vma=False,
    )
```
